128 devices in a mesh: region: 16 (over y_hi, z, core), tp: 8 (over y_lo, x).
Axes of the slice: x: 4, y: 4 (y_hi: 2, y_lo: 2; y = y_hi * 2 + y_lo), z: 4, core: 2. Of those that a mesh axis runs over, the one named last changes fastest.
Arguments:
- hidden_states: bfloat16 [4096, 5120], P('region'), may hold values from -100 to 100
- qkv_master: float32 [5120, 8, 896], P(('region', 'tp')), may hold values from -0.078125 to 0.078125
- out_master: float32 [5120, 8, 640], P(('region', 'tp')), may hold values from -0.078125 to 0.078125
- qkv_bias: bfloat16 [8, 896], P('tp'), may hold values from -3 to 3
- key_cache: bfloat16 [4096, 8, 128, 128], P('region', 'tp'), may hold values from -2200 to 2200
- value_cache: bfloat16 [4096, 8, 128, 128], P('region', 'tp'), may hold values from -6 to 6
- lengths: int32 [4096], P('region'), may hold values from 4 to 128, as said below
Outputs:
- attn_output: bfloat16 [4096, 5120], P('region', 'tp')
The draws below stay inside these ranges and needn't reach their ends.
Inputs may be any that keep to these rules, and one draw needn't show every extreme that they name: `lengths`: the largest length is 128.
All inputs are finite; a program needn't handle non-finite values.
Results may differ from the reference program's by a relative error of at most 0.019.
The reference program's roundings to bfloat16 on the way count: a program that leaves them out, or rounds other values in their place, can miss the bound.
Values may be sent and summed in bfloat16 or wider, within the bound.
A program may use at most 192 MiB of HBM per device.

```python
import math
import jax
import jax.numpy as jnp
from jax import lax

D = 5120
QHEADS = 40
KVH = 8
HD = 128
QBLOCK = 128
SEQS = 256
CACHE = 128
QPG = 5
GW = 896
QW = 640
ALL_SEQS = 4096
N_REGION = 16


def draw_hidden_states(key, part):
    first, second, third = jax.random.split(key, 3)
    base = jax.random.normal(first, (ALL_SEQS, D), jnp.float32)
    base = jnp.clip(base, -5.0, 5.0)
    row_scale = jnp.exp(jax.random.uniform(second, (ALL_SEQS, 1), jnp.float32, 0.0, math.log(10.0)))
    col_scale = jnp.exp(jax.random.uniform(third, (1, D), jnp.float32, 0.0, math.log(10.0)))
    return (0.2 * base * row_scale * col_scale).astype(jnp.bfloat16)


def draw_key_cache(key, part):
    first = jax.random.fold_in(key, 0)
    base = jnp.clip(jax.random.normal(first, (ALL_SEQS, KVH, CACHE, HD), jnp.float32), -5.0, 5.0)
    return base.astype(jnp.bfloat16)


def draw_lengths(key, part):
    first, second = jax.random.split(key, 2)
    values = jax.random.randint(first, (ALL_SEQS,), 4, CACHE + 1)
    where_full = jax.random.randint(second, (), 0, ALL_SEQS)
    return values.at[where_full].set(CACHE).astype(jnp.int32)


def block_scale(rng, shape, shards, least, high):
    def one(dim, shards_of):
        draws = jax.random.uniform(jax.random.fold_in(jax.random.fold_in(rng, 6), dim), (shards_of,), jnp.float32, least / len(shards), high / len(shards))
        return jnp.repeat(jnp.exp(draws), shape[dim] // shards_of).reshape((-1,) + (1,) * (len(shape) - dim - 1))

    factor_of = one(*shards[0])
    for cut in shards[1:]:
        factor_of = factor_of * one(*cut)
    return factor_of


def centred(stream_key, extent, deviation, bound, cuts=(), kind=jnp.bfloat16):
    gain = block_scale(stream_key, extent, cuts, -0.22, 0.18) if cuts else 1.0
    values = jax.random.normal(stream_key, extent, jnp.float32) * deviation * gain
    return jnp.minimum(jnp.maximum(values, -bound), bound).astype(kind)


def setup_inputs(seed: int = 0) -> dict:
    splits = jax.random.split(jax.random.key(seed), 8)
    return {
        "hidden_states": draw_hidden_states(jax.random.fold_in(splits[7], 71), 0),
        "qkv_master": centred(splits[1], (D, KVH, GW), D ** -0.5, 0.078125, ((0, 128),), jnp.float32),
        "out_master": centred(splits[2], (D, KVH, QW), (QHEADS * HD) ** -0.5, 0.078125, ((0, 128),), jnp.float32),
        "qkv_bias": centred(splits[3], (KVH, GW), 0.5, 3.0, ((0, 8),)),
        "key_cache": draw_key_cache(jax.random.fold_in(splits[7], 71), 0),
        "value_cache": centred(splits[5], (ALL_SEQS, KVH, CACHE, HD), 1.0, 6.0, ((0, 16), (1, 8))),
        "lengths": draw_lengths(jax.random.fold_in(splits[7], 71), 0),
    }


rope_base = 1000000.0

def restore_master(master):
    row_count, group_count, width = master.shape
    blocks = master.reshape(row_count, group_count, width // QBLOCK, QBLOCK)
    largest = lax.optimization_barrier(jnp.max(jnp.abs(blocks), axis=3, keepdims=True))
    scales = (largest + 1e-06).astype(jnp.bfloat16)
    scales = lax.optimization_barrier(scales)
    scale_wide = scales.astype(jnp.float32)
    codes = (blocks / scale_wide).astype(jnp.bfloat16)
    codes = lax.optimization_barrier(codes)
    return (codes.astype(jnp.float32) * scale_wide).astype(jnp.bfloat16).reshape(master.shape)

def rotate(values, angles):
    half_dim = values.shape[-1] // 2
    cosine = jnp.concatenate([jnp.cos(angles), jnp.cos(angles)], axis=-1)
    sine = jnp.concatenate([jnp.sin(angles), jnp.sin(angles)], axis=-1)
    turned = jnp.concatenate([-values[..., half_dim:], values[..., :half_dim]], axis=-1)
    return values * cosine + turned * sine

def attend(block):
    query, key_new, value_new, key_block, value_block, length_block = block
    inv_root = 1.0 / jnp.sqrt(jnp.float32(HD))
    query_wide = query.astype(jnp.float32)
    cache_scores = jnp.einsum('sgjd,sgcd->sgjc', query_wide, key_block.astype(jnp.float32)) * inv_root
    self_scores = jnp.einsum('sgjd,sgd->sgj', query_wide, key_new.astype(jnp.float32)) * inv_root
    slots = jnp.arange(key_block.shape[2], dtype=jnp.int32)
    valid_mask = (slots[None, :] < length_block[:, None])[:, None, None, :]
    cache_scores = jnp.where(valid_mask, cache_scores, -1e+30)
    peak_score = jnp.maximum(lax.optimization_barrier(jnp.max(cache_scores, axis=-1)), self_scores)
    cache_exp = jnp.where(valid_mask, jnp.exp(cache_scores - peak_score[..., None]), 0.0)
    self_exp = jnp.exp(self_scores - peak_score)
    denominator = lax.optimization_barrier(jnp.sum(cache_exp, axis=-1)) + self_exp
    cache_probs = (cache_exp / denominator[..., None]).astype(jnp.bfloat16)
    self_probs = (self_exp / denominator).astype(jnp.bfloat16)
    attended = jnp.einsum('sgjc,sgcd->sgjd', cache_probs.astype(jnp.float32), value_block.astype(jnp.float32))
    attended = attended + self_probs.astype(jnp.float32)[..., None] * value_new.astype(jnp.float32)[:, :, None, :]
    return attended.astype(jnp.bfloat16)

def reference(hidden_states, qkv_master, out_master, qkv_bias, key_cache, value_cache, lengths):
    qkv_weight = restore_master(qkv_master)
    out_weight = restore_master(out_master)
    widened = hidden_states.astype(jnp.float32)
    normed = widened * lax.rsqrt(lax.optimization_barrier(jnp.mean(widened * widened, axis=1, keepdims=True)) + 1e-06)
    normed = normed.astype(jnp.bfloat16)
    projected = jnp.dot(normed, qkv_weight.reshape(D, KVH * GW), preferred_element_type=jnp.float32)
    projected = projected.reshape(ALL_SEQS, KVH, GW) + qkv_bias.astype(jnp.float32)
    query = projected[..., :QW].reshape(ALL_SEQS, KVH, QPG, HD)
    key_new = projected[..., QW:QW + HD]
    value_new = projected[..., QW + HD:]
    frequency = rope_base ** (-jnp.arange(0, HD, 2, dtype=jnp.float32) / HD)
    angles = lengths.astype(jnp.float32)[:, None] * frequency[None, :]
    query = rotate(query, angles[:, None, None, :]).astype(jnp.bfloat16)
    key_new = rotate(key_new, angles[:, None, :]).astype(jnp.bfloat16)
    value_new = value_new.astype(jnp.bfloat16)

    def split_regions(array):
        return array.reshape((N_REGION, SEQS) + array.shape[1:])
    blocks = (split_regions(query), split_regions(key_new), split_regions(value_new), split_regions(key_cache), split_regions(value_cache), split_regions(lengths))
    attended = lax.map(attend, blocks).reshape(ALL_SEQS, KVH * QW)
    result = lax.dot_general(attended, out_weight.reshape(D, KVH * QW), (((1,), (1,)), ((), ())), preferred_element_type=jnp.float32)
    return result.astype(jnp.bfloat16)
```

```python
import functools

import jax
import jax.numpy as jnp
import numpy as np
from jax import lax
from jax.experimental import pallas as pl
from jax.experimental.pallas import tpu as pltpu
from jax.sharding import PartitionSpec as P

HD = 128
QPG = 5
NH = 2
NZ = 4
NX = 4
ROWS = 40
GW = 896
QW = 640
SEQS = 256
CACHE = 128
D = 5120
UQ = 8 * ROWS
UO = 4 * ROWS
ROPE_BASE = 1000000.0
MESH = pl.DeviceIdType.MESH
NSEM = 160
ABLK = 32

PIECES = {"q": ((0, 160), (160, 160)), "o": ((0, 80), (80, 80))}


def restore(block):
    largest = jnp.max(jnp.abs(block), axis=1, keepdims=True)
    scale = (largest + 1e-06).astype(jnp.bfloat16).astype(jnp.float32)
    codes = (block / scale).astype(jnp.bfloat16).astype(jnp.float32)
    return (codes * scale).astype(jnp.bfloat16)


def kernel(
    hid_hbm, qm_hbm, om_hbm, bias_ref, kc_hbm, vc_hbm, lens_ref, freq_ref, out_ref,
    qm, om, hid, normed, kc, vc, sq, so, wq, wo, acc, qs, kn, vn, atf, at2, pbuf, rsbuf,
    ld_sem, send_sem, recv_sem,
):
    region = lax.axis_index("region")
    t = lax.axis_index("tp")
    c = lax.rem(region, 2)
    z = lax.rem(region // 2, NZ)
    h = region // (2 * NZ)
    x = lax.rem(t, NX)
    lo = t // NX

    def dev(hh, zz, cc, ll, xx):
        return ((hh * NZ + zz) * 2 + cc, ll * NX + xx)

    zp, zm, z2 = lax.rem(z + 1, NZ), lax.rem(z + 3, NZ), lax.rem(z + 2, NZ)
    zrel = {0: z, 1: zp, -1: zm, 2: z2}
    hrel = {0: h, 1: 1 - h}
    sib = dev(h, z, 1 - c, lo, x)
    ypart = dev(1 - h, z, c, lo, x)
    up = dev(h, zp, c, lo, x)
    down = dev(h, zm, c, lo, x)
    swapped = [dev(lo, z, c, h, lax.rem(x + d, NX)) for d in range(NX)]
    mirrored = h == lo

    def columns(src, dst, first):
        return [
            pltpu.make_async_copy(
                src.at[:, pl.ds(128 * b, 128)], dst.at[b], ld_sem.at[first + b]
            )
            for b in range(dst.shape[0])
        ]

    q_loads, o_loads = columns(qm_hbm, qm, 6), columns(om_hbm, om, 13)
    loads = [
        None,
        None,
        pltpu.make_async_copy(hid_hbm, hid, ld_sem.at[2]),
        pltpu.make_async_copy(kc_hbm, kc, ld_sem.at[3]),
        pltpu.make_async_copy(vc_hbm, vc, ld_sem.at[4]),
    ]
    for copy in (*q_loads, *o_loads, loads[2]):
        copy.start()

    barrier = pltpu.get_barrier_semaphore()

    def greet(device):
        pl.semaphore_signal(barrier, inc=1, device_id=device, device_id_type=MESH)

    for k in range(1, 8):
        greet((region, lax.rem(t + k, 8)))
    for device in (sib, ypart, up, down):
        greet(device)

    @pl.when(jnp.logical_not(mirrored))
    def _():
        for device in swapped:
            greet(device)

    recv_at, pending = {}, []

    def rsem(key):
        return recv_sem.at[recv_at.setdefault(key, len(recv_at))]

    def send(src, dst, key, device):
        copy = pltpu.make_async_remote_copy(
            src_ref=src, dst_ref=dst, send_sem=send_sem.at[len(pending)], recv_sem=rsem(key),
            device_id=device, device_id_type=MESH,
        )
        pending.append(copy)
        copy.start()

    def arrived(view, key):
        pltpu.make_async_remote_copy(
            src_ref=view, dst_ref=view, send_sem=send_sem.at[0], recv_sem=rsem(key),
            device_id=sib, device_id_type=MESH,
        ).wait_recv()

    for copy in q_loads:
        copy.wait()

    def quant_q(g, carry):
        for b in range(GW // 128):
            block = qm[b, pl.ds(g, ROWS, stride=8), :]
            sq[g, :, pl.ds(128 * b, 128)] = restore(block)
        return carry

    lax.fori_loop(0, 8, quant_q, 0)

    pl.semaphore_wait(barrier, jnp.where(mirrored, 11, 15))

    home = h * NZ + z
    mine = pl.ds(pl.multiple_of(c * UQ + t * ROWS, 8), ROWS)
    for k in (4, 1, 3, 5, 7, 2, 6):
        other = lax.rem(t + k, 8)
        send(sq.at[other], wq.at[home, mine], ("aq", k), (region, other))
    own = pltpu.make_async_copy(sq.at[t], wq.at[home, mine], ld_sem.at[5])
    own.start()

    for copy in o_loads:
        copy.wait()

    def quant_o(xx, carry):
        for ll in range(2):
            for b in range(QW // 128):
                block = om[b, pl.ds(ll * NX + xx, ROWS, stride=8), :]
                so[xx, :, pl.ds(ll * QW + 128 * b, 128)] = restore(block)
        return carry

    lax.fori_loop(0, NX, quant_o, 0)

    loads[3].start()
    loads[4].start()

    loads[2].wait()

    def norm_rows(i, carry):
        rows = pl.ds(pl.multiple_of(i * 16, 16), 16)
        total = jnp.zeros((16, 128), jnp.float32)
        for b in range(D // 128):
            v = hid[rows, pl.ds(128 * b, 128)].astype(jnp.float32)
            total = total + v * v
        inv = lax.rsqrt(jnp.sum(total, axis=1, keepdims=True) / D + 1e-06)
        for b in range(8):
            v = hid[rows, pl.ds(640 * b, 640)].astype(jnp.float32)
            normed[b, rows, :] = (v * inv).astype(jnp.bfloat16)
        return carry

    lax.fori_loop(0, SEQS // 16, norm_rows, 0)

    def view(m, dh, dz, piece, part, core):
        off, rows = PIECES[m][piece]
        if part == 1:
            rows = rows // 2
        elif part == 2:
            off, rows = off + rows // 2, rows // 2
        if m == "q":
            base = core * UQ + off
            return wq.at[hrel[dh] * NZ + zrel[dz], pl.ds(pl.multiple_of(base, 8), rows)]
        base = core * 2 * UO + hrel[dh] * UO + off
        return wo.at[zrel[dz], pl.ds(pl.multiple_of(base, 8), rows)]

    def push(m, p, dh, dz, part, device, dz_there, dh_there, part_key):
        v = view(m, dh, dz, p, part, c)
        send(v, v, (m, p, dh_there, dz_there, part_key), device)

    def share(m, p, dh, dz, part):
        v = view(m, dh, dz, p, part, c)
        send(v, v, ("s", m, p, dh, dz, part), sib)

    def start_own(m, p):
        push(m, p, 0, 0, 0, ypart, 0, 1, 0)
        push(m, p, 0, 0, 0, up, -1, 0, 0)
        push(m, p, 0, 0, 0, down, 1, 0, 0)
        share(m, p, 0, 0, 0)

    def arrive(m, p, dh, dz, part=0):
        arrived(view(m, dh, dz, p, part, c), (m, p, dh, dz, part))
        if dz == 0:
            push(m, p, 1, 0, 0, up, -1, 1, 0)
            push(m, p, 1, 0, 0, down, 1, 1, 0)
        elif dz == -1:
            push(m, p, dh, -1, 1, up, 2, dh, 1)
        elif dz == 1:
            push(m, p, dh, 1, 2, down, 2, dh, 2)
        share(m, p, dh, dz, part)

    def shared(m, dh, dz):
        for p in range(len(PIECES[m])):
            for part in (1, 2) if dz == 2 else (0,):
                arrived(view(m, dh, dz, p, part, 1 - c), ("s", m, p, dh, dz, part))

    def multiply(dh, dz, first=False):
        shared("q", dh, dz)
        b = hrel[dh] * NZ + zrel[dz]
        for n in range(2):
            cols = pl.ds(512 * n, 512 if n == 0 else GW - 512)
            prod = jnp.dot(normed[b], wq[b, :, cols], preferred_element_type=jnp.float32)
            if first:
                acc[:, cols] = prod
            else:
                acc[:, cols] += prod

    own.wait()
    for k in range(1, 8):
        src = lax.rem(t + 8 - k, 8)
        arrived(wq.at[home, pl.ds(pl.multiple_of(c * UQ + src * ROWS, 8), ROWS)], ("aq", k))
    start_own("q", 0)
    start_own("q", 1)
    for p in range(2):
        arrive("q", p, 1, 0)
        arrive("q", p, 0, -1)
        arrive("q", p, 0, 1)
    multiply(0, 0, first=True)
    multiply(1, 0)

    place = pl.ds(pl.multiple_of(c * 2 * UO + lo * UO + x * ROWS, 8), ROWS)
    for d in (1, 3, 2):
        send(so.at[lax.rem(x + d, NX)], wo.at[z, place], ("ao", d), swapped[d])
    straight = pltpu.make_async_remote_copy(
        src_ref=so.at[x], dst_ref=wo.at[z, place], send_sem=send_sem.at[NSEM - 1],
        recv_sem=rsem(("ao", 0)), device_id=swapped[0], device_id_type=MESH,
    )

    @pl.when(mirrored)
    def _():
        pltpu.make_async_copy(so.at[x], wo.at[z, place], rsem(("ao", 0))).start()

    @pl.when(jnp.logical_not(mirrored))
    def _():
        straight.start()

    multiply(0, -1)
    multiply(0, 1)
    for p in range(2):
        arrive("q", p, 1, -1)
        arrive("q", p, 1, 1)
    for d in range(NX):
        src = lax.rem(x + NX - d, NX)
        where = pl.ds(pl.multiple_of(c * 2 * UO + h * UO + src * ROWS, 8), ROWS)
        arrived(wo.at[z, where], ("ao", d))
    start_own("o", 0)
    start_own("o", 1)
    multiply(1, -1)
    multiply(1, 1)
    for dh in (0, 1):
        for p in range(2):
            arrive("q", p, dh, 2, 1)
            arrive("q", p, dh, 2, 2)
        multiply(dh, 2)

    angles = lens_ref[...].astype(jnp.float32) * freq_ref[...]
    cosine = jnp.cos(angles)
    lane = lax.broadcasted_iota(jnp.int32, (SEQS, HD), 1)
    sine = jnp.where(lane < HD // 2, -jnp.sin(angles), jnp.sin(angles))

    def rounded(v):
        return v.astype(jnp.bfloat16).astype(jnp.float32)

    def projected(j):
        cols = pl.ds(HD * j, HD)
        return acc[:, cols] + bias_ref[:, cols].astype(jnp.float32)

    def rotate(u):
        return rounded(u * cosine + pltpu.roll(u, HD // 2, 1) * sine)

    for j in range(QPG):
        qs[pl.ds(j, SEQS, stride=8), :] = rotate(projected(j))
    for j in range(QPG, 8):
        qs[pl.ds(j, SEQS, stride=8), :] = jnp.zeros((SEQS, HD), jnp.float32)
    kn[...] = rotate(projected(QPG))
    vn[...] = rounded(projected(QPG + 1))

    loads[3].wait()
    loads[4].wait()
    inv_root = np.float32(1.0) / np.sqrt(np.float32(HD))

    def attend(i, carry):
        rows = pl.ds(pl.multiple_of(i * ABLK, ABLK), ABLK)
        rows8 = pl.ds(pl.multiple_of(i * ABLK * 8, ABLK * 8), ABLK * 8)
        q = qs[rows8, :].reshape(ABLK, 8, HD)
        scores = jnp.einsum(
            "bqd,bkd->bqk", q.astype(jnp.bfloat16), kc[rows], preferred_element_type=jnp.float32
        ) * inv_root
        self_scores = jnp.sum(q * kn[rows, :][:, None, :], axis=-1, keepdims=True) * inv_root
        slot = lax.broadcasted_iota(jnp.int32, (ABLK, 8, CACHE), 2)
        valid = slot < jnp.broadcast_to(lens_ref[rows, :][:, None, :], (ABLK, 8, CACHE))
        scores = jnp.where(valid, scores, -1e30)
        peak = jnp.maximum(jnp.max(scores, axis=-1, keepdims=True), self_scores)
        e = jnp.where(valid, jnp.exp(scores - peak), 0.0)
        self_e = jnp.exp(self_scores - peak)
        den = jnp.sum(e, axis=-1, keepdims=True) + self_e
        probs = (e / den).astype(jnp.bfloat16)
        self_p = rounded(self_e / den)
        out = jnp.einsum("bqk,bkd->bqd", probs, vc[rows], preferred_element_type=jnp.float32)
        out = out + self_p * vn[rows, :][:, None, :]
        atf[...] = out.reshape(ABLK * 8, HD)
        for j in range(QPG):
            head = atf[pl.ds(j, ABLK, stride=8), :]
            at2[lo, rows, pl.ds(HD * j, HD)] = head.astype(jnp.bfloat16)
        return carry

    def attend_range(a, b):
        lax.fori_loop(a, b, attend, 0)

    pair = (region, lax.rem(t + NX, 2 * NX))

    def exchange(k):
        v = at2.at[lo, pl.ds(128 * k, 128)]
        send(v, v, ("at", k), pair)

    attend_range(0, 3)
    for p in range(2):
        arrive("o", p, 1, 0)
        arrive("o", p, 0, -1)
        arrive("o", p, 0, 1)
    attend_range(3, 5)
    exchange(0)
    attend_range(5, 8)
    exchange(1)
    for p in range(2):
        arrive("o", p, 1, -1)
        arrive("o", p, 1, 1)

    late = []

    def finish(dz):
        zb = zrel[dz]
        for dh in (0, 1):
            shared("o", dh, dz)
        prod = lax.dot_general(
            at2[0], wo[zb, :, pl.ds(0, QW)], (((1,), (1,)), ((), ())),
            preferred_element_type=jnp.float32,
        )
        prod = prod + lax.dot_general(
            at2[1], wo[zb, :, pl.ds(QW, QW)], (((1,), (1,)), ((), ())),
            preferred_element_type=jnp.float32,
        )
        pbuf[zb] = prod.astype(jnp.bfloat16)
        hop = lax.rem(zb - x + NX, NX)
        copy = pltpu.make_async_remote_copy(
            src_ref=pbuf.at[zb], dst_ref=rsbuf.at[hop], send_sem=send_sem.at[NSEM - 6 + dz],
            recv_sem=recv_sem.at[NSEM - 8 + hop], device_id=(region, lo * NX + zb),
            device_id_type=MESH,
        )
        late.append((zb, copy))

        @pl.when(zb != x)
        def _():
            copy.start()

    for k in range(2):
        arrived(at2.at[1 - lo, pl.ds(128 * k, 128)], ("at", k))
    finish(0)
    finish(-1)
    finish(1)
    for dh in (0, 1):
        for p in range(2):
            arrive("o", p, dh, 2, 1)
            arrive("o", p, dh, 2, 2)
    finish(2)

    total = pbuf[x].astype(jnp.float32)
    for hop in range(1, NX):
        pltpu.make_async_remote_copy(
            src_ref=rsbuf.at[hop], dst_ref=rsbuf.at[hop], send_sem=send_sem.at[0],
            recv_sem=recv_sem.at[NSEM - 8 + hop], device_id=sib, device_id_type=MESH,
        ).wait_recv()
        total = total + rsbuf[hop].astype(jnp.float32)
    out_ref[...] = total.astype(jnp.bfloat16)

    for copy in pending:
        copy.wait_send()

    @pl.when(jnp.logical_not(mirrored))
    def _():
        straight.wait_send()

    for zb, copy in late:

        @pl.when(zb != x)
        def _(copy=copy):
            copy.wait_send()

    assert len(pending) < NSEM - 10 and len(recv_at) < NSEM - 10


def body(hidden_states, qkv_master, out_master, qkv_bias, key_cache, value_cache, lengths):
    seqs = hidden_states.shape[0]
    lens = jnp.broadcast_to(lengths[:, None], (seqs, HD))
    half = np.arange(0, HD, 2, dtype=np.float64) / HD
    freq = np.tile(ROPE_BASE ** (-half), 2)[None, :].astype(np.float32)
    bf16, f32 = jnp.bfloat16, jnp.float32
    anywhere = pl.BlockSpec(memory_space=pl.ANY)
    local = pl.BlockSpec(memory_space=pltpu.VMEM)
    return pl.pallas_call(
        kernel,
        out_shape=jax.ShapeDtypeStruct((seqs, QW), bf16),
        in_specs=[anywhere, anywhere, anywhere, local, anywhere, anywhere, local, local],
        out_specs=local,
        scratch_shapes=[
            pltpu.VMEM((GW // 128, 8 * ROWS, 128), f32),
            pltpu.VMEM((QW // 128, 8 * ROWS, 128), f32),
            pltpu.VMEM((SEQS, D), bf16),
            pltpu.VMEM((8, SEQS, D // 8), bf16),
            pltpu.VMEM((SEQS, CACHE, HD), bf16),
            pltpu.VMEM((SEQS, CACHE, HD), bf16),
            pltpu.VMEM((8, ROWS, GW), bf16),
            pltpu.VMEM((NX, ROWS, 2 * QW), bf16),
            pltpu.VMEM((8, 2 * UQ, GW), bf16),
            pltpu.VMEM((NZ, 4 * UO, 2 * QW), bf16),
            pltpu.VMEM((SEQS, GW), f32),
            pltpu.VMEM((SEQS * 8, HD), f32),
            pltpu.VMEM((SEQS, HD), f32),
            pltpu.VMEM((SEQS, HD), f32),
            pltpu.VMEM((ABLK * 8, HD), f32),
            pltpu.VMEM((2, SEQS, QW), bf16),
            pltpu.VMEM((NX, SEQS, QW), bf16),
            pltpu.VMEM((NX, SEQS, QW), bf16),
            pltpu.SemaphoreType.DMA((18,)),
            pltpu.SemaphoreType.DMA((NSEM,)),
            pltpu.SemaphoreType.DMA((NSEM,)),
        ],
        compiler_params=pltpu.CompilerParams(
            collective_id=0, has_side_effects=True, vmem_limit_bytes=66 * 1024 * 1024 - 2**21
        ),
        name="sync_attend",
    )(
        hidden_states,
        qkv_master.reshape(8 * ROWS, GW),
        out_master.reshape(8 * ROWS, QW),
        qkv_bias,
        key_cache.reshape(SEQS, CACHE, HD),
        value_cache.reshape(SEQS, CACHE, HD),
        lens,
        jnp.asarray(freq),
    )


def solution(mesh):
    return jax.shard_map(
        body,
        mesh=mesh,
        in_specs=(
            P("region", None),
            P(("region", "tp"), None, None),
            P(("region", "tp"), None, None),
            P("tp", None),
            P("region", "tp", None, None),
            P("region", "tp", None, None),
            P("region"),
        ),
        out_specs=P("region", "tp"),
        check_vma=False,
    )
```

```python
import functools

import jax
import jax.numpy as jnp
import numpy as np
from jax import lax
from jax.experimental import pallas as pl
from jax.experimental.pallas import tpu as pltpu
from jax.sharding import PartitionSpec as P

HD = 128
QPG = 5
NH = 2
NZ = 4
NX = 4
ROWS = 40
GW = 896
QW = 640
SEQS = 256
CACHE = 128
D = 5120
UQ = 8 * ROWS
UO = 4 * ROWS
ROPE_BASE = 1000000.0
MESH = pl.DeviceIdType.MESH
NSEM = 256
ABLK = 32

QP = (("on", 0, 80, "A"), ("on", 80, 80, "B"), ("off", 0, 80, "D"), ("off", 80, 80, "D"))
OP = ((0, 80), (80, 80), (160, 80), (240, 80))
OHALF = 160


def restore(block):
    largest = jnp.max(jnp.abs(block), axis=1, keepdims=True)
    scale = (largest + 1e-06).astype(jnp.bfloat16).astype(jnp.float32)
    codes = (block / scale).astype(jnp.bfloat16).astype(jnp.float32)
    return (codes * scale).astype(jnp.bfloat16)


def kernel(
    hid_hbm, qm_hbm, om_hbm, bias_ref, kc_hbm, vc_hbm, lens_ref, freq_ref, out_ref,
    qm, om, hid, normed, kc, vc, sq, so, wq, wo, acc, qs, kn, vn, lensb, atf, at2, pbuf, rsbuf,
    ld_sem, send_sem, recv_sem,
):
    region = lax.axis_index("region")
    t = lax.axis_index("tp")
    c = lax.rem(region, 2)
    z = lax.rem(region // 2, NZ)
    h = region // (2 * NZ)
    x = lax.rem(t, NX)
    lo = t // NX

    def dev(hh, zz, cc, ll, xx):
        return ((hh * NZ + zz) * 2 + cc, ll * NX + xx)

    zp, zm, z2 = lax.rem(z + 1, NZ), lax.rem(z + 3, NZ), lax.rem(z + 2, NZ)
    zrel = {0: z, 1: zp, -1: zm, 2: z2}
    hrel = {0: h, 1: 1 - h}
    sib = dev(h, z, 1 - c, lo, x)
    ypart = dev(1 - h, z, c, lo, x)
    up = dev(h, zp, c, lo, x)
    down = dev(h, zm, c, lo, x)

    def columns(src, dst, first):
        return [
            pltpu.make_async_copy(
                src.at[:, pl.ds(128 * b, 128)], dst.at[b], ld_sem.at[first + b]
            )
            for b in range(dst.shape[0])
        ]

    q_loads, o_loads = columns(qm_hbm, qm, 6), columns(om_hbm, om, 13)
    loads = [
        None,
        None,
        pltpu.make_async_copy(hid_hbm, hid, ld_sem.at[2]),
        pltpu.make_async_copy(kc_hbm, kc, ld_sem.at[3]),
        pltpu.make_async_copy(vc_hbm, vc, ld_sem.at[4]),
    ]
    for copy in (*q_loads, *o_loads, loads[2]):
        copy.start()

    barrier = pltpu.get_barrier_semaphore()

    def greet(device):
        pl.semaphore_signal(barrier, inc=1, device_id=device, device_id_type=MESH)

    for dh in (0, 1):
        for dl in (0, 1):
            for dx in range(NX):
                if (dh, dl, dx) != (0, 0, 0):
                    greet(dev(hrel[dh], z, c, lo if dl == 0 else 1 - lo, lax.rem(x + dx, NX)))
    for device in (sib, up, down):
        greet(device)

    recv_at, pending = {}, []

    def rsem(key):
        return recv_sem.at[recv_at.setdefault(key, len(recv_at))]

    def send(src, dst, key, device):
        copy = pltpu.make_async_remote_copy(
            src_ref=src, dst_ref=dst, send_sem=send_sem.at[len(pending)], recv_sem=rsem(key),
            device_id=device, device_id_type=MESH,
        )
        pending.append(copy)
        copy.start()

    def landed(view, sem_at):
        pltpu.make_async_remote_copy(
            src_ref=view, dst_ref=view, send_sem=send_sem.at[0], recv_sem=recv_sem.at[sem_at],
            device_id=sib, device_id_type=MESH,
        ).wait_recv()

    def arrived(view, key):
        landed(view, recv_at.setdefault(key, len(recv_at)))

    for copy in q_loads:
        copy.wait()

    def quant_q(k, carry):
        for b in range(GW // 128):
            block = qm[b, pl.ds(k, ROWS, stride=8), :]
            sq[k, :, pl.ds(128 * b, 128)] = restore(block)
        return carry

    def group_sems(count, key):
        first = len(recv_at)
        for i in range(count):
            recv_at[(key, i)] = first + i
        return first

    on_sem = group_sems(NX, "on")
    off_sem = group_sems(2 * NX, "off")
    ao_sem = group_sems(2 * NX, "ao")

    def scatter(src, dst, sem_at, device):
        copy = pltpu.make_async_remote_copy(
            src_ref=src, dst_ref=dst, send_sem=send_sem.at[len(pending)],
            recv_sem=recv_sem.at[sem_at], device_id=device, device_id_type=MESH,
        )
        pending.append(copy)
        copy.start()

    lax.fori_loop(lo * NX, lo * NX + NX, quant_q, 0)
    pl.semaphore_wait(barrier, 18)

    home = h * NZ + z
    mine = pl.ds(pl.multiple_of(c * UQ + t * ROWS, 8), ROWS)
    for dx in (1, 3, 2):
        xx = lax.rem(x + dx, NX)
        scatter(sq.at[lo * NX + xx], wq.at[home, mine], on_sem + x, dev(h, z, c, lo, xx))
    pltpu.make_async_copy(sq.at[t], wq.at[home, mine], recv_sem.at[on_sem + x]).start()

    lax.fori_loop((1 - lo) * NX, (1 - lo) * NX + NX, quant_q, 0)
    for dx in (0, 1, 3, 2):
        xx = lax.rem(x + dx, NX)
        for dh in (0, 1):
            scatter(
                sq.at[(1 - lo) * NX + xx], wq.at[home, mine], off_sem + NX * dh + x,
                dev(hrel[dh], z, c, 1 - lo, xx),
            )

    for copy in o_loads:
        copy.wait()

    def quant_o(xx, carry):
        for ll in range(2):
            for b in range(QW // 128):
                block = om[b, pl.ds(ll * NX + xx, ROWS, stride=8), :]
                so[xx, :, pl.ds(ll * QW + 128 * b, 128)] = restore(block)
        return carry

    lax.fori_loop(0, NX, quant_o, 0)

    loads[3].start()
    loads[4].start()

    loads[2].wait()

    def norm_rows(i, carry):
        rows = pl.ds(pl.multiple_of(i * 16, 16), 16)
        total = jnp.zeros((16, 128), jnp.float32)
        for b in range(D // 128):
            v = hid[rows, pl.ds(128 * b, 128)].astype(jnp.float32)
            total = total + v * v
        inv = lax.rsqrt(jnp.sum(total, axis=1, keepdims=True) / D + 1e-06)
        for b in range(8):
            v = hid[rows, pl.ds(640 * b, 640)].astype(jnp.float32)
            normed[b, rows, :] = (v * inv).astype(jnp.bfloat16)
        return carry

    lax.fori_loop(0, SEQS // 16, norm_rows, 0)

    lensb[...] = jnp.concatenate(
        [
            jnp.broadcast_to(lens_ref[pl.ds(i, 1), :].astype(jnp.float32), (HD, HD)).T
            for i in range(SEQS // HD)
        ],
        axis=0,
    )

    def part_of(off, rows, part):
        if part:
            return off + (rows // 2) * (part - 1), rows // 2
        return off, rows

    def qview(p, dh, dz, part=0, core=c):
        parity, off, rows, _ = QP[p]
        off, rows = part_of(off, rows, part)
        base = core * UQ + (lo if parity == "on" else 1 - lo) * (UQ // 2) + off
        return wq.at[hrel[dh] * NZ + zrel[dz], pl.ds(pl.multiple_of(base, 8), rows)]

    def oview(p, dz, part=0, core=c):
        off, rows = part_of(*OP[p], part)
        return wo.at[zrel[dz], pl.ds(pl.multiple_of(core * 2 * UO + off, 8), rows)]

    def move(v, key, device):
        send(v, v, key, device)

    def qready(p):
        parity, off, rows, route = QP[p]
        for dh in (0,) if parity == "on" else (0, 1):
            for src in range(off // ROWS, (off + rows) // ROWS):
                sem_at = on_sem + src if parity == "on" else off_sem + NX * dh + src
                base = c * UQ + (lo if parity == "on" else 1 - lo) * (UQ // 2) + src * ROWS
                v = wq.at[hrel[dh] * NZ + z, pl.ds(pl.multiple_of(base, 8), ROWS)]
                landed(v, sem_at)
            v = qview(p, dh, 0)
            move(v, ("q", p, dh, -1, 0), up)
            move(v, ("q", p, dh, 1, 0), down)
            move(v, ("qs", p, dh, 0, 0), sib)
            if route != "D":
                move(v, ("q", p, 1, 0, 0), ypart)

    def qarrive(p, dh, dz):
        route = QP[p][3]
        for part in (1, 2) if dz == 2 else (0,):
            v = qview(p, dh, dz, part)
            arrived(v, ("q", p, dh, dz, part))
            if dz == -1 and (route != "A" or dh == 0):
                move(qview(p, dh, dz, 1), ("q", p, dh, 2, 1), up)
            if dz == 1 and (route != "A" or dh == 0):
                move(qview(p, dh, dz, 2), ("q", p, dh, 2, 2), down)
            if route == "A" and dh == 0:
                move(v, ("q", p, 1, dz, part), ypart)
            if route == "B" and dz == 0:
                move(v, ("q", p, 1, -1, 0), up)
                move(v, ("q", p, 1, 1, 0), down)
            move(v, ("qs", p, dh, dz, part), sib)

    def multiply(dh, dz, first=False):
        for p in range(len(QP)):
            for part in (1, 2) if dz == 2 else (0,):
                arrived(qview(p, dh, dz, part, 1 - c), ("qs", p, dh, dz, part))
        b = hrel[dh] * NZ + zrel[dz]
        for n in range(2):
            cols = pl.ds(512 * n, 512 if n == 0 else GW - 512)
            prod = jnp.dot(normed[b], wq[b, :, cols], preferred_element_type=jnp.float32)
            if first:
                acc[:, cols] = prod
            else:
                acc[:, cols] += prod

    def oready(p):
        off, rows = OP[p]
        for src in range(off // ROWS, (off + rows) // ROWS):
            base = c * 2 * UO + src * ROWS
            landed(wo.at[z, pl.ds(pl.multiple_of(base, 8), ROWS)], ao_sem + src)
        v = oview(p, 0)
        move(v, ("o", p, -1, 0), up)
        move(v, ("o", p, 1, 0), down)
        move(v, ("os", p, 0, 0), sib)

    def oarrive(p, dz):
        for part in (1, 2) if dz == 2 else (0,):
            v = oview(p, dz, part)
            arrived(v, ("o", p, dz, part))
            if dz == -1:
                move(oview(p, dz, 1), ("o", p, 2, 1), up)
            if dz == 1:
                move(oview(p, dz, 2), ("o", p, 2, 2), down)
            move(v, ("os", p, dz, part), sib)

    qready(0)
    qready(1)
    qready(2)
    qarrive(0, 0, -1)
    qarrive(0, 0, 1)
    qarrive(1, 1, 0)
    qready(3)
    qarrive(1, 0, -1)
    qarrive(1, 0, 1)

    place = pl.ds(pl.multiple_of(c * 2 * UO + lo * UO + x * ROWS, 8), ROWS)
    to_self = []
    for dx in (0, 1, 3, 2):
        xx = lax.rem(x + dx, NX)
        for hh in (0, 1):
            if dx:
                scatter(so.at[xx], wo.at[z, place], ao_sem + NX * lo + x, dev(hh, z, c, h, xx))
                continue
            away = jnp.logical_or(h != hh, lo != h)
            copy = pltpu.make_async_remote_copy(
                src_ref=so.at[xx], dst_ref=wo.at[z, place], send_sem=send_sem.at[NSEM - 1 - hh],
                recv_sem=recv_sem.at[ao_sem + NX * lo + x], device_id=dev(hh, z, c, h, xx),
                device_id_type=MESH,
            )
            to_self.append((away, copy))

            @pl.when(away)
            def _(copy=copy):
                copy.start()

    @pl.when(h == lo)
    def _():
        pltpu.make_async_copy(
            so.at[x], wo.at[z, place], recv_sem.at[ao_sem + NX * lo + x]
        ).start()

    multiply(0, 0, first=True)
    qarrive(0, 0, 2)
    for dh in (0, 1):
        qarrive(2, dh, -1)
        qarrive(2, dh, 1)
    qarrive(1, 1, -1)
    qarrive(1, 1, 1)
    for dh in (0, 1):
        qarrive(3, dh, -1)
        qarrive(3, dh, 1)
    oready(0)
    oready(1)
    multiply(0, -1)
    multiply(0, 1)
    qarrive(0, 1, 0)
    qarrive(0, 1, -1)
    qarrive(0, 1, 1)
    oready(2)
    oready(3)
    multiply(1, 0)
    qarrive(0, 1, 2)
    qarrive(1, 0, 2)
    qarrive(2, 0, 2)
    qarrive(3, 0, 2)
    multiply(1, -1)
    multiply(1, 1)
    qarrive(1, 1, 2)
    qarrive(2, 1, 2)
    qarrive(3, 1, 2)
    multiply(0, 2)
    multiply(1, 2)

    angles = lensb[...] * freq_ref[...]
    cosine = jnp.cos(angles)
    lane = lax.broadcasted_iota(jnp.int32, (SEQS, HD), 1)
    sine = jnp.where(lane < HD // 2, -jnp.sin(angles), jnp.sin(angles))

    def rounded(v):
        return v.astype(jnp.bfloat16).astype(jnp.float32)

    def projected(j):
        cols = pl.ds(HD * j, HD)
        return acc[:, cols] + bias_ref[:, cols].astype(jnp.float32)

    def rotate(u):
        return rounded(u * cosine + pltpu.roll(u, HD // 2, 1) * sine)

    for j in range(QPG):
        qs[pl.ds(j, SEQS, stride=8), :] = rotate(projected(j))
    for j in range(QPG, 8):
        qs[pl.ds(j, SEQS, stride=8), :] = jnp.zeros((SEQS, HD), jnp.float32)
    kn[...] = rotate(projected(QPG))
    vn[...] = rounded(projected(QPG + 1))

    loads[3].wait()
    loads[4].wait()
    inv_root = np.float32(1.0) / np.sqrt(np.float32(HD))

    def attend(i, carry):
        rows = pl.ds(pl.multiple_of(i * ABLK, ABLK), ABLK)
        rows8 = pl.ds(pl.multiple_of(i * ABLK * 8, ABLK * 8), ABLK * 8)
        q = qs[rows8, :].reshape(ABLK, 8, HD)
        scores = jnp.einsum(
            "bqd,bkd->bqk", q.astype(jnp.bfloat16), kc[rows], preferred_element_type=jnp.float32
        ) * inv_root
        self_scores = jnp.sum(q * kn[rows, :][:, None, :], axis=-1, keepdims=True) * inv_root
        slot = lax.broadcasted_iota(jnp.int32, (ABLK, 8, CACHE), 2).astype(jnp.float32)
        valid = slot < jnp.broadcast_to(lensb[rows, :][:, None, :], (ABLK, 8, CACHE))
        scores = jnp.where(valid, scores, -1e30)
        peak = jnp.maximum(jnp.max(scores, axis=-1, keepdims=True), self_scores)
        e = jnp.where(valid, jnp.exp(scores - peak), 0.0)
        self_e = jnp.exp(self_scores - peak)
        den = jnp.sum(e, axis=-1, keepdims=True) + self_e
        probs = (e / den).astype(jnp.bfloat16)
        self_p = rounded(self_e / den)
        out = jnp.einsum("bqk,bkd->bqd", probs, vc[rows], preferred_element_type=jnp.float32)
        out = out + self_p * vn[rows, :][:, None, :]
        atf[...] = out.reshape(ABLK * 8, HD)
        for j in range(QPG):
            head = atf[pl.ds(j, ABLK, stride=8), :]
            at2[lo, rows, pl.ds(HD * j, HD)] = head.astype(jnp.bfloat16)
        return carry

    def attend_range(a, b):
        lax.fori_loop(a, b, attend, 0)

    pair = (region, lax.rem(t + NX, 2 * NX))

    def exchange(k):
        v = at2.at[lo, pl.ds(128 * k, 128)]
        send(v, v, ("at", k), pair)

    attend_range(0, 2)
    oarrive(0, -1)
    oarrive(0, 1)
    attend_range(2, 4)
    exchange(0)
    oarrive(1, -1)
    oarrive(1, 1)
    attend_range(4, 6)
    oarrive(2, -1)
    oarrive(2, 1)
    attend_range(6, 8)
    exchange(1)
    oarrive(3, -1)
    oarrive(3, 1)
    for k in range(2):
        arrived(at2.at[1 - lo, pl.ds(128 * k, 128)], ("at", k))

    late = []
    hop_sem = group_sems(NX * 4, "hop")
    per = OHALF // OP[0][1]

    def finish(dz, side, half):
        core = c if side == 0 else 1 - c
        zb = zrel[dz]
        for p in range(per * half, per * half + per):
            for part in (1, 2) if dz == 2 else (0,):
                if side == 1:
                    arrived(oview(p, dz, part, core), ("os", p, dz, part))
        rows = pl.ds(pl.multiple_of(core * 2 * UO + half * OHALF, 32), OHALF)
        prod = jnp.zeros((OHALF, SEQS), jnp.float32)
        for ll in range(2):
            prod = prod + lax.dot_general(
                wo[zb, rows, pl.ds(QW * ll, QW)], at2[ll], (((1,), (1,)), ((), ())),
                preferred_element_type=jnp.float32,
            )
        pbuf[zb, rows, :] = prod.astype(jnp.bfloat16)
        hop = lax.rem(zb - x + NX, NX)
        copy = pltpu.make_async_remote_copy(
            src_ref=pbuf.at[zb, rows], dst_ref=rsbuf.at[hop, rows],
            send_sem=send_sem.at[NSEM - 3 - len(late)],
            recv_sem=recv_sem.at[hop_sem + 4 * hop + 2 * side + half],
            device_id=dev(h, z, c, lo, zb), device_id_type=MESH,
        )
        late.append((zb, copy))

        @pl.when(zb != x)
        def _():
            copy.start()

    for dz in (0, -1, 1):
        for side in (0, 1):
            for half in (0, 1):
                finish(dz, side, half)
    for p in range(4):
        oarrive(p, 2)
    for half in (0, 1):
        for side in (0, 1):
            finish(2, side, half)

    total = pbuf[x].astype(jnp.float32)
    for hop in range(1, NX):
        for side in (0, 1):
            core = c if side == 0 else 1 - c
            for half in (0, 1):
                rows = pl.ds(pl.multiple_of(core * 2 * UO + half * OHALF, 32), OHALF)
                landed(rsbuf.at[hop, rows], hop_sem + 4 * hop + 2 * side + half)
        total = total + rsbuf[hop].astype(jnp.float32)
    out_ref[...] = total.T.astype(jnp.bfloat16)

    for copy in pending:
        copy.wait_send()

    for away, copy in to_self:

        @pl.when(away)
        def _(copy=copy):
            copy.wait_send()

    for zb, copy in late:

        @pl.when(zb != x)
        def _(copy=copy):
            copy.wait_send()

    assert len(pending) < NSEM - 20 and len(recv_at) <= NSEM


def body(hidden_states, qkv_master, out_master, qkv_bias, key_cache, value_cache, lengths):
    seqs = hidden_states.shape[0]
    lens = lengths.reshape(seqs // HD, HD)
    half = np.arange(0, HD, 2, dtype=np.float64) / HD
    freq = np.tile(ROPE_BASE ** (-half), 2)[None, :].astype(np.float32)
    bf16, f32 = jnp.bfloat16, jnp.float32
    anywhere = pl.BlockSpec(memory_space=pl.ANY)
    local = pl.BlockSpec(memory_space=pltpu.VMEM)
    return pl.pallas_call(
        kernel,
        out_shape=jax.ShapeDtypeStruct((seqs, QW), bf16),
        in_specs=[anywhere, anywhere, anywhere, local, anywhere, anywhere, local, local],
        out_specs=local,
        scratch_shapes=[
            pltpu.VMEM((GW // 128, 8 * ROWS, 128), f32),
            pltpu.VMEM((QW // 128, 8 * ROWS, 128), f32),
            pltpu.VMEM((SEQS, D), bf16),
            pltpu.VMEM((8, SEQS, D // 8), bf16),
            pltpu.VMEM((SEQS, CACHE, HD), bf16),
            pltpu.VMEM((SEQS, CACHE, HD), bf16),
            pltpu.VMEM((8, ROWS, GW), bf16),
            pltpu.VMEM((NX, ROWS, 2 * QW), bf16),
            pltpu.VMEM((8, 2 * UQ, GW), bf16),
            pltpu.VMEM((NZ, 4 * UO, 2 * QW), bf16),
            pltpu.VMEM((SEQS, GW), f32),
            pltpu.VMEM((SEQS * 8, HD), f32),
            pltpu.VMEM((SEQS, HD), f32),
            pltpu.VMEM((SEQS, HD), f32),
            pltpu.VMEM((SEQS, HD), f32),
            pltpu.VMEM((ABLK * 8, HD), f32),
            pltpu.VMEM((2, SEQS, QW), bf16),
            pltpu.VMEM((NX, QW, SEQS), bf16),
            pltpu.VMEM((NX, QW, SEQS), bf16),
            pltpu.SemaphoreType.DMA((18,)),
            pltpu.SemaphoreType.DMA((NSEM,)),
            pltpu.SemaphoreType.DMA((NSEM,)),
        ],
        compiler_params=pltpu.CompilerParams(
            collective_id=0, has_side_effects=True, vmem_limit_bytes=66 * 1024 * 1024 - 2**21
        ),
        name="sync_attend",
    )(
        hidden_states,
        qkv_master.reshape(8 * ROWS, GW),
        out_master.reshape(8 * ROWS, QW),
        qkv_bias,
        key_cache.reshape(SEQS, CACHE, HD),
        value_cache.reshape(SEQS, CACHE, HD),
        lens,
        jnp.asarray(freq),
    )


def solution(mesh):
    return jax.shard_map(
        body,
        mesh=mesh,
        in_specs=(
            P("region", None),
            P(("region", "tp"), None, None),
            P(("region", "tp"), None, None),
            P("tp", None),
            P("region", "tp", None, None),
            P("region", "tp", None, None),
            P("region"),
        ),
        out_specs=P("region", "tp"),
        check_vma=False,
    )
```

```python
import functools

import jax
import jax.numpy as jnp
import numpy as np
from jax import lax
from jax.experimental import pallas as pl
from jax.experimental.pallas import tpu as pltpu
from jax.sharding import PartitionSpec as P

HD = 128
QPG = 5
NH = 2
NZ = 4
NX = 4
ROWS = 40
GW = 896
QW = 640
SEQS = 256
CACHE = 128
D = 5120
UQ = 8 * ROWS
UO = 4 * ROWS
ROPE_BASE = 1000000.0
MESH = pl.DeviceIdType.MESH
NSEM = 256
ABLK = 32

QP = (("on", 0, 80, "A"), ("on", 80, 80, "B"), ("off", 0, 80, "D"), ("off", 80, 80, "D"))
OP = ((0, 80), (80, 80), (160, 80), (240, 80))


def restore(block):
    largest = jnp.max(jnp.abs(block), axis=1, keepdims=True)
    scale = (largest + 1e-06).astype(jnp.bfloat16).astype(jnp.float32)
    codes = (block / scale).astype(jnp.bfloat16).astype(jnp.float32)
    return (codes * scale).astype(jnp.bfloat16)


def kernel(
    hid_hbm, qm_hbm, om_hbm, bias_ref, kc_hbm, vc_hbm, lens_ref, freq_ref, out_ref,
    qm, om, hid, normed, kc, vc, sq, so, wq, wo, acc, qs, kn, vn, lensb, atf, at2, pbuf, rsbuf,
    ld_sem, send_sem, recv_sem,
):
    region = lax.axis_index("region")
    t = lax.axis_index("tp")
    c = lax.rem(region, 2)
    z = lax.rem(region // 2, NZ)
    h = region // (2 * NZ)
    x = lax.rem(t, NX)
    lo = t // NX

    def dev(hh, zz, cc, ll, xx):
        return ((hh * NZ + zz) * 2 + cc, ll * NX + xx)

    zp, zm, z2 = lax.rem(z + 1, NZ), lax.rem(z + 3, NZ), lax.rem(z + 2, NZ)
    zrel = {0: z, 1: zp, -1: zm, 2: z2}
    hrel = {0: h, 1: 1 - h}
    sib = dev(h, z, 1 - c, lo, x)
    ypart = dev(1 - h, z, c, lo, x)
    up = dev(h, zp, c, lo, x)
    down = dev(h, zm, c, lo, x)

    def columns(src, dst, first):
        return [
            pltpu.make_async_copy(
                src.at[:, pl.ds(128 * b, 128)], dst.at[b], ld_sem.at[first + b]
            )
            for b in range(dst.shape[0])
        ]

    q_loads, o_loads = columns(qm_hbm, qm, 6), columns(om_hbm, om, 13)
    loads = [
        None,
        None,
        pltpu.make_async_copy(hid_hbm, hid, ld_sem.at[2]),
        pltpu.make_async_copy(kc_hbm, kc, ld_sem.at[3]),
        pltpu.make_async_copy(vc_hbm, vc, ld_sem.at[4]),
    ]
    for copy in (*q_loads, *o_loads, loads[2]):
        copy.start()

    barrier = pltpu.get_barrier_semaphore()

    def greet(device):
        pl.semaphore_signal(barrier, inc=1, device_id=device, device_id_type=MESH)

    for dh in (0, 1):
        for dl in (0, 1):
            for dx in range(NX):
                if (dh, dl, dx) != (0, 0, 0):
                    greet(dev(hrel[dh], z, c, lo if dl == 0 else 1 - lo, lax.rem(x + dx, NX)))
    for device in (sib, up, down):
        greet(device)

    recv_at, pending = {}, []

    def rsem(key):
        return recv_sem.at[recv_at.setdefault(key, len(recv_at))]

    def send(src, dst, key, device):
        copy = pltpu.make_async_remote_copy(
            src_ref=src, dst_ref=dst, send_sem=send_sem.at[len(pending)], recv_sem=rsem(key),
            device_id=device, device_id_type=MESH,
        )
        pending.append(copy)
        copy.start()

    def landed(view, sem_at):
        pltpu.make_async_remote_copy(
            src_ref=view, dst_ref=view, send_sem=send_sem.at[0], recv_sem=recv_sem.at[sem_at],
            device_id=sib, device_id_type=MESH,
        ).wait_recv()

    def arrived(view, key):
        landed(view, recv_at.setdefault(key, len(recv_at)))

    for copy in q_loads:
        copy.wait()

    def quant_q(k, carry):
        for b in range(GW // 128):
            block = qm[b, pl.ds(k, ROWS, stride=8), :]
            sq[k, :, pl.ds(128 * b, 128)] = restore(block)
        return carry

    def group_sems(count, key):
        first = len(recv_at)
        for i in range(count):
            recv_at[(key, i)] = first + i
        return first

    on_sem = group_sems(NX, "on")
    off_sem = group_sems(2 * NX, "off")
    ao_sem = group_sems(2 * NX, "ao")

    def scatter(src, dst, sem_at, device):
        copy = pltpu.make_async_remote_copy(
            src_ref=src, dst_ref=dst, send_sem=send_sem.at[len(pending)],
            recv_sem=recv_sem.at[sem_at], device_id=device, device_id_type=MESH,
        )
        pending.append(copy)
        copy.start()

    lax.fori_loop(lo * NX, lo * NX + NX, quant_q, 0)
    pl.semaphore_wait(barrier, 18)

    home = h * NZ + z
    mine = pl.ds(pl.multiple_of(c * UQ + t * ROWS, 8), ROWS)
    for dx in (1, 3, 2):
        xx = lax.rem(x + dx, NX)
        scatter(sq.at[lo * NX + xx], wq.at[home, mine], on_sem + x, dev(h, z, c, lo, xx))
    pltpu.make_async_copy(sq.at[t], wq.at[home, mine], recv_sem.at[on_sem + x]).start()

    lax.fori_loop((1 - lo) * NX, (1 - lo) * NX + NX, quant_q, 0)
    for dx in (0, 1, 3, 2):
        xx = lax.rem(x + dx, NX)
        for dh in (0, 1):
            scatter(
                sq.at[(1 - lo) * NX + xx], wq.at[home, mine], off_sem + NX * dh + x,
                dev(hrel[dh], z, c, 1 - lo, xx),
            )

    for copy in o_loads:
        copy.wait()

    def quant_o(xx, carry):
        for ll in range(2):
            for b in range(QW // 128):
                block = om[b, pl.ds(ll * NX + xx, ROWS, stride=8), :]
                so[xx, :, pl.ds(ll * QW + 128 * b, 128)] = restore(block)
        return carry

    lax.fori_loop(0, NX, quant_o, 0)

    loads[3].start()
    loads[4].start()

    loads[2].wait()

    def norm_rows(i, carry):
        rows = pl.ds(pl.multiple_of(i * 16, 16), 16)
        total = jnp.zeros((16, 128), jnp.float32)
        for b in range(D // 128):
            v = hid[rows, pl.ds(128 * b, 128)].astype(jnp.float32)
            total = total + v * v
        inv = lax.rsqrt(jnp.sum(total, axis=1, keepdims=True) / D + 1e-06)
        for b in range(8):
            v = hid[rows, pl.ds(640 * b, 640)].astype(jnp.float32)
            normed[b, rows, :] = (v * inv).astype(jnp.bfloat16)
        return carry

    lax.fori_loop(0, SEQS // 16, norm_rows, 0)

    lensb[...] = jnp.concatenate(
        [
            jnp.broadcast_to(lens_ref[pl.ds(i, 1), :].astype(jnp.float32), (HD, HD)).T
            for i in range(SEQS // HD)
        ],
        axis=0,
    )

    def part_of(off, rows, part):
        if part:
            return off + (rows // 2) * (part - 1), rows // 2
        return off, rows

    def qview(p, dh, dz, part=0, core=c):
        parity, off, rows, _ = QP[p]
        off, rows = part_of(off, rows, part)
        base = core * UQ + (lo if parity == "on" else 1 - lo) * (UQ // 2) + off
        return wq.at[hrel[dh] * NZ + zrel[dz], pl.ds(pl.multiple_of(base, 8), rows)]

    def oview(p, dz, part=0, core=c):
        off, rows = part_of(*OP[p], part)
        return wo.at[zrel[dz], pl.ds(pl.multiple_of(core * 2 * UO + off, 8), rows)]

    def move(v, key, device):
        send(v, v, key, device)

    def qready(p):
        parity, off, rows, route = QP[p]
        for dh in (0,) if parity == "on" else (0, 1):
            for src in range(off // ROWS, (off + rows) // ROWS):
                sem_at = on_sem + src if parity == "on" else off_sem + NX * dh + src
                base = c * UQ + (lo if parity == "on" else 1 - lo) * (UQ // 2) + src * ROWS
                v = wq.at[hrel[dh] * NZ + z, pl.ds(pl.multiple_of(base, 8), ROWS)]
                landed(v, sem_at)
            v = qview(p, dh, 0)
            move(v, ("q", p, dh, -1, 0), up)
            move(v, ("q", p, dh, 1, 0), down)
            move(v, ("qs", p, dh, 0, 0), sib)
            if route != "D":
                move(v, ("q", p, 1, 0, 0), ypart)

    def qarrive(p, dh, dz):
        route = QP[p][3]
        for part in (1, 2) if dz == 2 else (0,):
            v = qview(p, dh, dz, part)
            arrived(v, ("q", p, dh, dz, part))
            if dz == -1 and (route != "A" or dh == 0):
                move(qview(p, dh, dz, 1), ("q", p, dh, 2, 1), up)
            if dz == 1 and (route != "A" or dh == 0):
                move(qview(p, dh, dz, 2), ("q", p, dh, 2, 2), down)
            if route == "A" and dh == 0:
                move(v, ("q", p, 1, dz, part), ypart)
            if route == "B" and dz == 0:
                move(v, ("q", p, 1, -1, 0), up)
                move(v, ("q", p, 1, 1, 0), down)
            move(v, ("qs", p, dh, dz, part), sib)

    def multiply(dh, dz, first=False):
        for p in range(len(QP)):
            for part in (1, 2) if dz == 2 else (0,):
                arrived(qview(p, dh, dz, part, 1 - c), ("qs", p, dh, dz, part))
        b = hrel[dh] * NZ + zrel[dz]
        for n in range(2):
            cols = pl.ds(512 * n, 512 if n == 0 else GW - 512)
            prod = jnp.dot(normed[b], wq[b, :, cols], preferred_element_type=jnp.float32)
            if first:
                acc[:, cols] = prod
            else:
                acc[:, cols] += prod

    def oready(p):
        off, rows = OP[p]
        for src in range(off // ROWS, (off + rows) // ROWS):
            base = c * 2 * UO + src * ROWS
            landed(wo.at[z, pl.ds(pl.multiple_of(base, 8), ROWS)], ao_sem + src)
        v = oview(p, 0)
        move(v, ("o", p, -1, 0), up)
        move(v, ("o", p, 1, 0), down)
        move(v, ("os", p, 0, 0), sib)

    def oarrive(p, dz):
        for part in (1, 2) if dz == 2 else (0,):
            v = oview(p, dz, part)
            arrived(v, ("o", p, dz, part))
            if dz == -1:
                move(oview(p, dz, 1), ("o", p, 2, 1), up)
            if dz == 1:
                move(oview(p, dz, 2), ("o", p, 2, 2), down)
            move(v, ("os", p, dz, part), sib)

    qready(0)
    qready(1)
    qready(2)
    qarrive(0, 0, -1)
    qarrive(0, 0, 1)
    qarrive(1, 1, 0)
    qready(3)
    qarrive(1, 0, -1)
    qarrive(1, 0, 1)

    place = pl.ds(pl.multiple_of(c * 2 * UO + lo * UO + x * ROWS, 8), ROWS)
    to_self = []
    for dx in (0, 1, 3, 2):
        xx = lax.rem(x + dx, NX)
        for hh in (0, 1):
            if dx:
                scatter(so.at[xx], wo.at[z, place], ao_sem + NX * lo + x, dev(hh, z, c, h, xx))
                continue
            away = jnp.logical_or(h != hh, lo != h)
            copy = pltpu.make_async_remote_copy(
                src_ref=so.at[xx], dst_ref=wo.at[z, place], send_sem=send_sem.at[NSEM - 1 - hh],
                recv_sem=recv_sem.at[ao_sem + NX * lo + x], device_id=dev(hh, z, c, h, xx),
                device_id_type=MESH,
            )
            to_self.append((away, copy))

            @pl.when(away)
            def _(copy=copy):
                copy.start()

    @pl.when(h == lo)
    def _():
        pltpu.make_async_copy(
            so.at[x], wo.at[z, place], recv_sem.at[ao_sem + NX * lo + x]
        ).start()

    multiply(0, 0, first=True)
    qarrive(0, 0, 2)
    for dh in (0, 1):
        qarrive(2, dh, -1)
        qarrive(2, dh, 1)
    qarrive(1, 1, -1)
    qarrive(1, 1, 1)
    for dh in (0, 1):
        qarrive(3, dh, -1)
        qarrive(3, dh, 1)
    oready(0)
    oready(1)
    multiply(0, -1)
    multiply(0, 1)
    qarrive(0, 1, 0)
    qarrive(0, 1, -1)
    qarrive(0, 1, 1)
    multiply(1, 0)
    qarrive(0, 1, 2)
    qarrive(1, 0, 2)
    qarrive(2, 0, 2)
    qarrive(3, 0, 2)
    multiply(1, -1)
    multiply(1, 1)
    qarrive(1, 1, 2)
    qarrive(2, 1, 2)
    qarrive(3, 1, 2)
    multiply(0, 2)
    multiply(1, 2)

    angles = lensb[...] * freq_ref[...]
    cosine = jnp.cos(angles)
    lane = lax.broadcasted_iota(jnp.int32, (SEQS, HD), 1)
    sine = jnp.where(lane < HD // 2, -jnp.sin(angles), jnp.sin(angles))

    def rounded(v):
        return v.astype(jnp.bfloat16).astype(jnp.float32)

    def projected(j):
        cols = pl.ds(HD * j, HD)
        return acc[:, cols] + bias_ref[:, cols].astype(jnp.float32)

    def rotate(u):
        return rounded(u * cosine + pltpu.roll(u, HD // 2, 1) * sine)

    for j in range(QPG):
        qs[pl.ds(j, SEQS, stride=8), :] = rotate(projected(j))
    for j in range(QPG, 8):
        qs[pl.ds(j, SEQS, stride=8), :] = jnp.zeros((SEQS, HD), jnp.float32)
    kn[...] = rotate(projected(QPG))
    vn[...] = rounded(projected(QPG + 1))

    loads[3].wait()
    loads[4].wait()
    inv_root = np.float32(1.0) / np.sqrt(np.float32(HD))

    def attend(i, carry):
        rows = pl.ds(pl.multiple_of(i * ABLK, ABLK), ABLK)
        rows8 = pl.ds(pl.multiple_of(i * ABLK * 8, ABLK * 8), ABLK * 8)
        q = qs[rows8, :].reshape(ABLK, 8, HD)
        scores = jnp.einsum(
            "bqd,bkd->bqk", q.astype(jnp.bfloat16), kc[rows], preferred_element_type=jnp.float32
        ) * inv_root
        self_scores = jnp.sum(q * kn[rows, :][:, None, :], axis=-1, keepdims=True) * inv_root
        slot = lax.broadcasted_iota(jnp.int32, (ABLK, 8, CACHE), 2).astype(jnp.float32)
        valid = slot < jnp.broadcast_to(lensb[rows, :][:, None, :], (ABLK, 8, CACHE))
        scores = jnp.where(valid, scores, -1e30)
        peak = jnp.maximum(jnp.max(scores, axis=-1, keepdims=True), self_scores)
        e = jnp.where(valid, jnp.exp(scores - peak), 0.0)
        self_e = jnp.exp(self_scores - peak)
        den = jnp.sum(e, axis=-1, keepdims=True) + self_e
        probs = (e / den).astype(jnp.bfloat16)
        self_p = rounded(self_e / den)
        out = jnp.einsum("bqk,bkd->bqd", probs, vc[rows], preferred_element_type=jnp.float32)
        out = out + self_p * vn[rows, :][:, None, :]
        atf[...] = out.reshape(ABLK * 8, HD)
        for j in range(QPG):
            head = atf[pl.ds(j, ABLK, stride=8), :]
            at2[lo, rows, pl.ds(HD * j, HD)] = head.astype(jnp.bfloat16)
        return carry

    def attend_range(a, b):
        lax.fori_loop(a, b, attend, 0)

    pair = (region, lax.rem(t + NX, 2 * NX))

    def exchange(k):
        v = at2.at[lo, pl.ds(128 * k, 128)]
        send(v, v, ("at", k), pair)

    late = []
    hop_sem = group_sems(NX * 8, "hop")
    np_ = len(OP)

    def finish(dz, side, first, count):
        core = c if side == 0 else 1 - c
        zb = zrel[dz]
        for p in range(first, first + count):
            for part in (1, 2) if dz == 2 else (0,):
                if side == 1:
                    arrived(oview(p, dz, part, core), ("os", p, dz, part))
        rows = pl.ds(
            pl.multiple_of(core * 2 * UO + OP[first][0], 16), OP[first][1] * count
        )
        prod = jnp.zeros((OP[first][1] * count, SEQS), jnp.float32)
        for ll in range(2):
            prod = prod + lax.dot_general(
                wo[zb, rows, pl.ds(QW * ll, QW)], at2[ll], (((1,), (1,)), ((), ())),
                preferred_element_type=jnp.float32,
            )
        pbuf[zb, rows, :] = prod.astype(jnp.bfloat16)
        hop = lax.rem(zb - x + NX, NX)
        copies = []
        for p in range(first, first + count):
            piece = pl.ds(pl.multiple_of(core * 2 * UO + OP[p][0], 16), OP[p][1])
            copies.append(
                pltpu.make_async_remote_copy(
                    src_ref=pbuf.at[zb, piece], dst_ref=rsbuf.at[hop, piece],
                    send_sem=send_sem.at[NSEM - 3 - len(late)],
                    recv_sem=recv_sem.at[hop_sem + 8 * hop + np_ * side + p],
                    device_id=dev(h, z, c, lo, zb), device_id_type=MESH,
                )
            )
            late.append((zb, copies[-1]))

        @pl.when(zb != x)
        def _():
            for copy in copies:
                copy.start()

    def both(dz, first, count):
        for side in (0, 1):
            finish(dz, side, first, count)

    attend_range(0, 2)
    oarrive(0, -1)
    oarrive(0, 1)
    oready(2)
    attend_range(2, 4)
    exchange(0)
    oarrive(1, -1)
    oarrive(1, 1)
    oready(3)
    attend_range(4, 6)
    oarrive(0, 2)
    attend_range(6, 8)
    exchange(1)
    oarrive(2, -1)
    oarrive(2, 1)
    for k in range(2):
        arrived(at2.at[1 - lo, pl.ds(128 * k, 128)], ("at", k))
    both(0, 0, 2)
    both(0, 2, 2)
    both(-1, 0, 2)
    both(1, 0, 2)
    oarrive(1, 2)
    both(2, 0, 2)
    oarrive(3, -1)
    oarrive(3, 1)
    both(-1, 2, 2)
    both(1, 2, 2)
    oarrive(2, 2)
    both(2, 2, 1)
    oarrive(3, 2)
    both(2, 3, 1)

    total = pbuf[x].astype(jnp.float32)
    for hop in range(1, NX):
        for side in (0, 1):
            core = c if side == 0 else 1 - c
            for p, (off, count) in enumerate(OP):
                rows = pl.ds(pl.multiple_of(core * 2 * UO + off, 16), count)
                landed(rsbuf.at[hop, rows], hop_sem + 8 * hop + np_ * side + p)
        total = total + rsbuf[hop].astype(jnp.float32)
    out_ref[...] = total.T.astype(jnp.bfloat16)

    for copy in pending:
        copy.wait_send()

    for away, copy in to_self:

        @pl.when(away)
        def _(copy=copy):
            copy.wait_send()

    for zb, copy in late:

        @pl.when(zb != x)
        def _(copy=copy):
            copy.wait_send()

    assert len(pending) < NSEM - 40 and len(recv_at) <= NSEM


def body(hidden_states, qkv_master, out_master, qkv_bias, key_cache, value_cache, lengths):
    seqs = hidden_states.shape[0]
    lens = lengths.reshape(seqs // HD, HD)
    half = np.arange(0, HD, 2, dtype=np.float64) / HD
    freq = np.tile(ROPE_BASE ** (-half), 2)[None, :].astype(np.float32)
    bf16, f32 = jnp.bfloat16, jnp.float32
    anywhere = pl.BlockSpec(memory_space=pl.ANY)
    local = pl.BlockSpec(memory_space=pltpu.VMEM)
    return pl.pallas_call(
        kernel,
        out_shape=jax.ShapeDtypeStruct((seqs, QW), bf16),
        in_specs=[anywhere, anywhere, anywhere, local, anywhere, anywhere, local, local],
        out_specs=local,
        scratch_shapes=[
            pltpu.VMEM((GW // 128, 8 * ROWS, 128), f32),
            pltpu.VMEM((QW // 128, 8 * ROWS, 128), f32),
            pltpu.VMEM((SEQS, D), bf16),
            pltpu.VMEM((8, SEQS, D // 8), bf16),
            pltpu.VMEM((SEQS, CACHE, HD), bf16),
            pltpu.VMEM((SEQS, CACHE, HD), bf16),
            pltpu.VMEM((8, ROWS, GW), bf16),
            pltpu.VMEM((NX, ROWS, 2 * QW), bf16),
            pltpu.VMEM((8, 2 * UQ, GW), bf16),
            pltpu.VMEM((NZ, 4 * UO, 2 * QW), bf16),
            pltpu.VMEM((SEQS, GW), f32),
            pltpu.VMEM((SEQS * 8, HD), f32),
            pltpu.VMEM((SEQS, HD), f32),
            pltpu.VMEM((SEQS, HD), f32),
            pltpu.VMEM((SEQS, HD), f32),
            pltpu.VMEM((ABLK * 8, HD), f32),
            pltpu.VMEM((2, SEQS, QW), bf16),
            pltpu.VMEM((NX, QW, SEQS), bf16),
            pltpu.VMEM((NX, QW, SEQS), bf16),
            pltpu.SemaphoreType.DMA((18,)),
            pltpu.SemaphoreType.DMA((NSEM,)),
            pltpu.SemaphoreType.DMA((NSEM,)),
        ],
        compiler_params=pltpu.CompilerParams(
            collective_id=0, has_side_effects=True, vmem_limit_bytes=66 * 1024 * 1024 - 2**21
        ),
        name="sync_attend",
    )(
        hidden_states,
        qkv_master.reshape(8 * ROWS, GW),
        out_master.reshape(8 * ROWS, QW),
        qkv_bias,
        key_cache.reshape(SEQS, CACHE, HD),
        value_cache.reshape(SEQS, CACHE, HD),
        lens,
        jnp.asarray(freq),
    )


def solution(mesh):
    return jax.shard_map(
        body,
        mesh=mesh,
        in_specs=(
            P("region", None),
            P(("region", "tp"), None, None),
            P(("region", "tp"), None, None),
            P("tp", None),
            P("region", "tp", None, None),
            P("region", "tp", None, None),
            P("region"),
        ),
        out_specs=P("region", "tp"),
        check_vma=False,
    )
```

```python
import functools

import jax
import jax.numpy as jnp
import numpy as np
from jax import lax
from jax.experimental import pallas as pl
from jax.experimental.pallas import tpu as pltpu
from jax.sharding import PartitionSpec as P

HD = 128
QPG = 5
NH = 2
NZ = 4
NX = 4
ROWS = 40
GW = 896
QW = 640
SEQS = 256
CACHE = 128
D = 5120
UQ = 8 * ROWS
UO = 4 * ROWS
ROPE_BASE = 1000000.0
MESH = pl.DeviceIdType.MESH
NSEM = 256
ABLK = 32

QP = (("on", 0, 80, "B"), ("on", 80, 80, "B"), ("off", 0, 80, "D"), ("off", 80, 80, "D"))
OP = ((0, 80), (80, 80), (160, 80), (240, 80))


def restore(block):
    largest = jnp.max(jnp.abs(block), axis=1, keepdims=True)
    scale = (largest + 1e-06).astype(jnp.bfloat16).astype(jnp.float32)
    codes = (block / scale).astype(jnp.bfloat16).astype(jnp.float32)
    return (codes * scale).astype(jnp.bfloat16)


def kernel(
    hid_hbm, qm_hbm, om_hbm, bias_ref, kc_hbm, vc_hbm, lens_ref, freq_ref, out_ref,
    qm, om, hid, normed, kc, vc, sq, so, wq, wo, acc, qs, kn, vn, lensb, atf, at2, att, pbuf, rsbuf,
    ld_sem, send_sem, recv_sem,
):
    region = lax.axis_index("region")
    t = lax.axis_index("tp")
    c = lax.rem(region, 2)
    z = lax.rem(region // 2, NZ)
    h = region // (2 * NZ)
    x = lax.rem(t, NX)
    lo = t // NX

    def dev(hh, zz, cc, ll, xx):
        return ((hh * NZ + zz) * 2 + cc, ll * NX + xx)

    zp, zm, z2 = lax.rem(z + 1, NZ), lax.rem(z + 3, NZ), lax.rem(z + 2, NZ)
    zrel = {0: z, 1: zp, -1: zm, 2: z2}
    hrel = {0: h, 1: 1 - h}
    sib = dev(h, z, 1 - c, lo, x)
    ypart = dev(1 - h, z, c, lo, x)
    up = dev(h, zp, c, lo, x)
    down = dev(h, zm, c, lo, x)

    def columns(src, dst, first):
        return [
            pltpu.make_async_copy(
                src.at[:, pl.ds(128 * b, 128)], dst.at[b], ld_sem.at[first + b]
            )
            for b in range(dst.shape[0])
        ]

    q_loads, o_loads = columns(qm_hbm, qm, 6), columns(om_hbm, om, 13)
    loads = [
        None,
        None,
        pltpu.make_async_copy(hid_hbm, hid, ld_sem.at[2]),
        pltpu.make_async_copy(kc_hbm, kc, ld_sem.at[3]),
        pltpu.make_async_copy(vc_hbm, vc, ld_sem.at[4]),
    ]
    for copy in (*q_loads, *o_loads, loads[2]):
        copy.start()

    barrier = pltpu.get_barrier_semaphore()

    def greet(device):
        pl.semaphore_signal(barrier, inc=1, device_id=device, device_id_type=MESH)

    for dh in (0, 1):
        for dl in (0, 1):
            for dx in range(NX):
                if (dh, dl, dx) != (0, 0, 0):
                    greet(dev(hrel[dh], z, c, lo if dl == 0 else 1 - lo, lax.rem(x + dx, NX)))
    for device in (sib, up, down):
        greet(device)

    recv_at, pending = {}, []

    def rsem(key):
        return recv_sem.at[recv_at.setdefault(key, len(recv_at))]

    def send(src, dst, key, device):
        copy = pltpu.make_async_remote_copy(
            src_ref=src, dst_ref=dst, send_sem=send_sem.at[len(pending)], recv_sem=rsem(key),
            device_id=device, device_id_type=MESH,
        )
        pending.append(copy)
        copy.start()

    def landed(view, sem_at):
        pltpu.make_async_remote_copy(
            src_ref=view, dst_ref=view, send_sem=send_sem.at[0], recv_sem=recv_sem.at[sem_at],
            device_id=sib, device_id_type=MESH,
        ).wait_recv()

    def arrived(view, key):
        landed(view, recv_at.setdefault(key, len(recv_at)))

    for copy in q_loads:
        copy.wait()

    def quant_q(k, carry):
        for b in range(GW // 128):
            block = qm[b, pl.ds(k, ROWS, stride=8), :]
            sq[k, :, pl.ds(128 * b, 128)] = restore(block)
        return carry

    def group_sems(count, key):
        first = len(recv_at)
        for i in range(count):
            recv_at[(key, i)] = first + i
        return first

    on_sem = group_sems(NX, "on")
    off_sem = group_sems(2 * NX, "off")
    ao_sem = group_sems(2 * NX, "ao")

    def scatter(src, dst, sem_at, device):
        copy = pltpu.make_async_remote_copy(
            src_ref=src, dst_ref=dst, send_sem=send_sem.at[len(pending)],
            recv_sem=recv_sem.at[sem_at], device_id=device, device_id_type=MESH,
        )
        pending.append(copy)
        copy.start()

    lax.fori_loop(lo * NX, lo * NX + NX, quant_q, 0)
    pl.semaphore_wait(barrier, 18)

    home = h * NZ + z
    mine = pl.ds(pl.multiple_of(c * UQ + t * ROWS, 8), ROWS)
    for dx in (1, 3, 2):
        xx = lax.rem(x + dx, NX)
        scatter(sq.at[lo * NX + xx], wq.at[home, mine], on_sem + x, dev(h, z, c, lo, xx))
    pltpu.make_async_copy(sq.at[t], wq.at[home, mine], recv_sem.at[on_sem + x]).start()

    lax.fori_loop((1 - lo) * NX, (1 - lo) * NX + NX, quant_q, 0)
    for dx in (0, 1, 3, 2):
        xx = lax.rem(x + dx, NX)
        for dh in (0, 1):
            scatter(
                sq.at[(1 - lo) * NX + xx], wq.at[home, mine], off_sem + NX * dh + x,
                dev(hrel[dh], z, c, 1 - lo, xx),
            )

    for copy in o_loads:
        copy.wait()

    def quant_o(xx, carry):
        for ll in range(2):
            for b in range(QW // 128):
                block = om[b, pl.ds(ll * NX + xx, ROWS, stride=8), :]
                so[xx, :, pl.ds(ll * QW + 128 * b, 128)] = restore(block)
        return carry

    lax.fori_loop(0, NX, quant_o, 0)

    loads[3].start()
    loads[4].start()

    loads[2].wait()

    def norm_rows(i, carry):
        rows = pl.ds(pl.multiple_of(i * 16, 16), 16)
        total = jnp.zeros((16, 128), jnp.float32)
        for b in range(D // 128):
            v = hid[rows, pl.ds(128 * b, 128)].astype(jnp.float32)
            total = total + v * v
        inv = lax.rsqrt(jnp.sum(total, axis=1, keepdims=True) / D + 1e-06)
        for b in range(8):
            v = hid[rows, pl.ds(640 * b, 640)].astype(jnp.float32)
            normed[b, rows, :] = (v * inv).astype(jnp.bfloat16)
        return carry

    lax.fori_loop(0, SEQS // 16, norm_rows, 0)

    lensb[...] = jnp.concatenate(
        [
            jnp.broadcast_to(lens_ref[pl.ds(i, 1), :].astype(jnp.float32), (HD, HD)).T
            for i in range(SEQS // HD)
        ],
        axis=0,
    )

    def part_of(off, rows, part):
        if part:
            return off + (rows // 2) * (part - 1), rows // 2
        return off, rows

    def qview(p, dh, dz, part=0, core=c):
        parity, off, rows, _ = QP[p]
        off, rows = part_of(off, rows, part)
        base = core * UQ + (lo if parity == "on" else 1 - lo) * (UQ // 2) + off
        return wq.at[hrel[dh] * NZ + zrel[dz], pl.ds(pl.multiple_of(base, 8), rows)]

    def oview(p, dz, part=0, core=c):
        off, rows = part_of(*OP[p], part)
        return wo.at[zrel[dz], pl.ds(pl.multiple_of(core * 2 * UO + off, 8), rows)]

    def move(v, key, device):
        send(v, v, key, device)

    def qready(p):
        parity, off, rows, route = QP[p]
        for dh in (0,) if parity == "on" else (0, 1):
            for src in range(off // ROWS, (off + rows) // ROWS):
                sem_at = on_sem + src if parity == "on" else off_sem + NX * dh + src
                base = c * UQ + (lo if parity == "on" else 1 - lo) * (UQ // 2) + src * ROWS
                v = wq.at[hrel[dh] * NZ + z, pl.ds(pl.multiple_of(base, 8), ROWS)]
                landed(v, sem_at)
            v = qview(p, dh, 0)
            move(v, ("q", p, dh, -1, 0), up)
            move(v, ("q", p, dh, 1, 0), down)
            move(v, ("qs", p, dh, 0, 0), sib)
            if route != "D":
                move(v, ("q", p, 1, 0, 0), ypart)

    def qarrive(p, dh, dz):
        route = QP[p][3]
        for part in (1, 2) if dz == 2 else (0,):
            v = qview(p, dh, dz, part)
            arrived(v, ("q", p, dh, dz, part))
            if dz == -1 and (route != "A" or dh == 0):
                move(qview(p, dh, dz, 1), ("q", p, dh, 2, 1), up)
            if dz == 1 and (route != "A" or dh == 0):
                move(qview(p, dh, dz, 2), ("q", p, dh, 2, 2), down)
            if route == "A" and dh == 0:
                move(v, ("q", p, 1, dz, part), ypart)
            if route == "B" and dz == 0:
                move(v, ("q", p, 1, -1, 0), up)
                move(v, ("q", p, 1, 1, 0), down)
            move(v, ("qs", p, dh, dz, part), sib)

    def multiply(dh, dz, first=False):
        for p in range(len(QP)):
            for part in (1, 2) if dz == 2 else (0,):
                arrived(qview(p, dh, dz, part, 1 - c), ("qs", p, dh, dz, part))
        b = hrel[dh] * NZ + zrel[dz]
        for n in range(2):
            cols = pl.ds(512 * n, 512 if n == 0 else GW - 512)
            prod = jnp.dot(normed[b], wq[b, :, cols], preferred_element_type=jnp.float32)
            if first:
                acc[:, cols] = prod
            else:
                acc[:, cols] += prod

    def oready(p):
        off, rows = OP[p]
        for src in range(off // ROWS, (off + rows) // ROWS):
            base = c * 2 * UO + src * ROWS
            landed(wo.at[z, pl.ds(pl.multiple_of(base, 8), ROWS)], ao_sem + src)
        v = oview(p, 0)
        move(v, ("o", p, -1, 0), up)
        move(v, ("o", p, 1, 0), down)
        move(v, ("os", p, 0, 0), sib)

    def oarrive(p, dz):
        for part in (1, 2) if dz == 2 else (0,):
            v = oview(p, dz, part)
            arrived(v, ("o", p, dz, part))
            if dz == -1:
                move(oview(p, dz, 1), ("o", p, 2, 1), up)
            if dz == 1:
                move(oview(p, dz, 2), ("o", p, 2, 2), down)
            move(v, ("os", p, dz, part), sib)

    qready(0)
    qready(1)
    qready(2)
    qarrive(0, 1, 0)
    qarrive(1, 1, 0)
    qready(3)
    qarrive(0, 0, -1)
    qarrive(0, 0, 1)
    qarrive(1, 0, -1)
    qarrive(1, 0, 1)
    multiply(0, 0, first=True)
    qarrive(0, 1, -1)
    qarrive(0, 1, 1)
    qarrive(2, 0, -1)
    qarrive(2, 0, 1)
    qarrive(2, 1, -1)
    qarrive(2, 1, 1)
    qarrive(1, 1, -1)
    qarrive(1, 1, 1)
    place = pl.ds(pl.multiple_of(c * 2 * UO + lo * UO + x * ROWS, 8), ROWS)
    to_self = []
    for dx in (0, 1, 3, 2):
        xx = lax.rem(x + dx, NX)
        for hh in (0, 1):
            if dx:
                scatter(so.at[xx], wo.at[z, place], ao_sem + NX * lo + x, dev(hh, z, c, h, xx))
                continue
            away = jnp.logical_or(h != hh, lo != h)
            copy = pltpu.make_async_remote_copy(
                src_ref=so.at[xx], dst_ref=wo.at[z, place], send_sem=send_sem.at[NSEM - 1 - hh],
                recv_sem=recv_sem.at[ao_sem + NX * lo + x], device_id=dev(hh, z, c, h, xx),
                device_id_type=MESH,
            )
            to_self.append((away, copy))

            @pl.when(away)
            def _(copy=copy):
                copy.start()

    @pl.when(h == lo)
    def _():
        pltpu.make_async_copy(
            so.at[x], wo.at[z, place], recv_sem.at[ao_sem + NX * lo + x]
        ).start()
    qarrive(3, 0, -1)
    qarrive(3, 0, 1)
    qarrive(3, 1, -1)
    qarrive(3, 1, 1)
    oready(0)
    oready(1)
    multiply(0, -1)
    multiply(0, 1)
    multiply(1, 0)
    qarrive(0, 0, 2)
    qarrive(1, 0, 2)
    qarrive(2, 0, 2)
    qarrive(3, 0, 2)
    multiply(1, -1)
    multiply(1, 1)
    qarrive(0, 1, 2)
    qarrive(1, 1, 2)
    qarrive(2, 1, 2)
    qarrive(3, 1, 2)
    multiply(0, 2)
    multiply(1, 2)

    angles = lensb[...] * freq_ref[...]
    cosine = jnp.cos(angles)
    lane = lax.broadcasted_iota(jnp.int32, (SEQS, HD), 1)
    sine = jnp.where(lane < HD // 2, -jnp.sin(angles), jnp.sin(angles))

    def rounded(v):
        return v.astype(jnp.bfloat16).astype(jnp.float32)

    def projected(j):
        cols = pl.ds(HD * j, HD)
        return acc[:, cols] + bias_ref[:, cols].astype(jnp.float32)

    def rotate(u):
        return rounded(u * cosine + pltpu.roll(u, HD // 2, 1) * sine)

    for j in range(QPG):
        qs[pl.ds(j, SEQS, stride=8), :] = rotate(projected(j))
    for j in range(QPG, 8):
        qs[pl.ds(j, SEQS, stride=8), :] = jnp.zeros((SEQS, HD), jnp.float32)
    kn[...] = rotate(projected(QPG))
    vn[...] = rounded(projected(QPG + 1))

    loads[3].wait()
    loads[4].wait()
    inv_root = np.float32(1.0) / np.sqrt(np.float32(HD))

    def attend(i, carry):
        rows = pl.ds(pl.multiple_of(i * ABLK, ABLK), ABLK)
        rows8 = pl.ds(pl.multiple_of(i * ABLK * 8, ABLK * 8), ABLK * 8)
        q = qs[rows8, :].reshape(ABLK, 8, HD)
        scores = jnp.einsum(
            "bqd,bkd->bqk", q.astype(jnp.bfloat16), kc[rows], preferred_element_type=jnp.float32
        ) * inv_root
        self_scores = jnp.sum(q * kn[rows, :][:, None, :], axis=-1, keepdims=True) * inv_root
        slot = lax.broadcasted_iota(jnp.int32, (ABLK, 8, CACHE), 2).astype(jnp.float32)
        valid = slot < jnp.broadcast_to(lensb[rows, :][:, None, :], (ABLK, 8, CACHE))
        scores = jnp.where(valid, scores, -1e30)
        peak = jnp.maximum(jnp.max(scores, axis=-1, keepdims=True), self_scores)
        e = jnp.where(valid, jnp.exp(scores - peak), 0.0)
        self_e = jnp.exp(self_scores - peak)
        den = jnp.sum(e, axis=-1, keepdims=True) + self_e
        probs = (e / den).astype(jnp.bfloat16)
        self_p = rounded(self_e / den)
        out = jnp.einsum("bqk,bkd->bqd", probs, vc[rows], preferred_element_type=jnp.float32)
        out = out + self_p * vn[rows, :][:, None, :]
        atf[...] = out.reshape(ABLK * 8, HD)
        for j in range(QPG):
            head = atf[pl.ds(j, ABLK, stride=8), :]
            at2[lo, rows, pl.ds(HD * j, HD)] = head.astype(jnp.bfloat16)
        return carry

    def attend_range(a, b):
        lax.fori_loop(a, b, attend, 0)

    pair = (region, lax.rem(t + NX, 2 * NX))

    def exchange(k):
        v = at2.at[lo, pl.ds(128 * k, 128)]
        send(v, v, ("at", k), pair)

    late = []
    hop_sem = group_sems(NX * 8, "hop")
    np_ = len(OP)

    def finish(dz, side, first, count):
        core = c if side == 0 else 1 - c
        zb = zrel[dz]
        for p in range(first, first + count):
            for part in (1, 2) if dz == 2 else (0,):
                if side == 1:
                    arrived(oview(p, dz, part, core), ("os", p, dz, part))
        rows = pl.ds(
            pl.multiple_of(core * 2 * UO + OP[first][0], 16), OP[first][1] * count
        )
        prod = jnp.zeros((OP[first][1] * count, SEQS), jnp.float32)
        for ll in range(2):
            prod = prod + jnp.dot(
                wo[zb, rows, pl.ds(QW * ll, QW)], att[ll], preferred_element_type=jnp.float32
            )
        pbuf[zb, rows, :] = prod.astype(jnp.bfloat16)
        hop = lax.rem(zb - x + NX, NX)
        copies = []
        for p in range(first, first + count):
            piece = pl.ds(pl.multiple_of(core * 2 * UO + OP[p][0], 16), OP[p][1])
            copies.append(
                pltpu.make_async_remote_copy(
                    src_ref=pbuf.at[zb, piece], dst_ref=rsbuf.at[hop, piece],
                    send_sem=send_sem.at[NSEM - 3 - len(late)],
                    recv_sem=recv_sem.at[hop_sem + 8 * hop + np_ * side + p],
                    device_id=dev(h, z, c, lo, zb), device_id_type=MESH,
                )
            )
            late.append((zb, copies[-1]))

        @pl.when(zb != x)
        def _():
            for copy in copies:
                copy.start()

    def both(dz, first, count):
        for side in (0, 1):
            finish(dz, side, first, count)

    attend_range(0, 2)
    oarrive(0, -1)
    oarrive(0, 1)
    oready(2)
    attend_range(2, 4)
    exchange(0)
    oarrive(1, -1)
    oarrive(1, 1)
    oready(3)
    attend_range(4, 6)
    oarrive(0, 2)
    attend_range(6, 8)
    exchange(1)
    oarrive(2, -1)
    oarrive(2, 1)
    for k in range(2):
        arrived(at2.at[1 - lo, pl.ds(128 * k, 128)], ("at", k))
        for ll in range(2):
            att[ll, :, pl.ds(128 * k, 128)] = at2[ll, pl.ds(128 * k, 128), :].T
    both(0, 0, 2)
    both(0, 2, 2)
    both(-1, 0, 2)
    both(1, 0, 2)
    oarrive(1, 2)
    both(2, 0, 2)
    oarrive(3, -1)
    oarrive(3, 1)
    both(-1, 2, 2)
    both(1, 2, 2)
    oarrive(2, 2)
    both(2, 2, 1)
    oarrive(3, 2)
    both(2, 3, 1)

    total = pbuf[x].astype(jnp.float32)
    for hop in range(1, NX):
        for side in (0, 1):
            core = c if side == 0 else 1 - c
            for p, (off, count) in enumerate(OP):
                rows = pl.ds(pl.multiple_of(core * 2 * UO + off, 16), count)
                landed(rsbuf.at[hop, rows], hop_sem + 8 * hop + np_ * side + p)
        total = total + rsbuf[hop].astype(jnp.float32)
    out_ref[...] = total.T.astype(jnp.bfloat16)

    for copy in pending:
        copy.wait_send()

    for away, copy in to_self:

        @pl.when(away)
        def _(copy=copy):
            copy.wait_send()

    for zb, copy in late:

        @pl.when(zb != x)
        def _(copy=copy):
            copy.wait_send()

    assert len(pending) < NSEM - 40 and len(recv_at) <= NSEM


def body(hidden_states, qkv_master, out_master, qkv_bias, key_cache, value_cache, lengths):
    seqs = hidden_states.shape[0]
    lens = lengths.reshape(seqs // HD, HD)
    half = np.arange(0, HD, 2, dtype=np.float64) / HD
    freq = np.tile(ROPE_BASE ** (-half), 2)[None, :].astype(np.float32)
    bf16, f32 = jnp.bfloat16, jnp.float32
    anywhere = pl.BlockSpec(memory_space=pl.ANY)
    local = pl.BlockSpec(memory_space=pltpu.VMEM)
    return pl.pallas_call(
        kernel,
        out_shape=jax.ShapeDtypeStruct((seqs, QW), bf16),
        in_specs=[anywhere, anywhere, anywhere, local, anywhere, anywhere, local, local],
        out_specs=local,
        scratch_shapes=[
            pltpu.VMEM((GW // 128, 8 * ROWS, 128), f32),
            pltpu.VMEM((QW // 128, 8 * ROWS, 128), f32),
            pltpu.VMEM((SEQS, D), bf16),
            pltpu.VMEM((8, SEQS, D // 8), bf16),
            pltpu.VMEM((SEQS, CACHE, HD), bf16),
            pltpu.VMEM((SEQS, CACHE, HD), bf16),
            pltpu.VMEM((8, ROWS, GW), bf16),
            pltpu.VMEM((NX, ROWS, 2 * QW), bf16),
            pltpu.VMEM((8, 2 * UQ, GW), bf16),
            pltpu.VMEM((NZ, 4 * UO, 2 * QW), bf16),
            pltpu.VMEM((SEQS, GW), f32),
            pltpu.VMEM((SEQS * 8, HD), f32),
            pltpu.VMEM((SEQS, HD), f32),
            pltpu.VMEM((SEQS, HD), f32),
            pltpu.VMEM((SEQS, HD), f32),
            pltpu.VMEM((ABLK * 8, HD), f32),
            pltpu.VMEM((2, SEQS, QW), bf16),
            pltpu.VMEM((2, QW, SEQS), bf16),
            pltpu.VMEM((NX, QW, SEQS), bf16),
            pltpu.VMEM((NX, QW, SEQS), bf16),
            pltpu.SemaphoreType.DMA((18,)),
            pltpu.SemaphoreType.DMA((NSEM,)),
            pltpu.SemaphoreType.DMA((NSEM,)),
        ],
        compiler_params=pltpu.CompilerParams(
            collective_id=0, has_side_effects=True, vmem_limit_bytes=66 * 1024 * 1024 - 2**21
        ),
        name="sync_attend",
    )(
        hidden_states,
        qkv_master.reshape(8 * ROWS, GW),
        out_master.reshape(8 * ROWS, QW),
        qkv_bias,
        key_cache.reshape(SEQS, CACHE, HD),
        value_cache.reshape(SEQS, CACHE, HD),
        lens,
        jnp.asarray(freq),
    )


def solution(mesh):
    return jax.shard_map(
        body,
        mesh=mesh,
        in_specs=(
            P("region", None),
            P(("region", "tp"), None, None),
            P(("region", "tp"), None, None),
            P("tp", None),
            P("region", "tp", None, None),
            P("region", "tp", None, None),
            P("region"),
        ),
        out_specs=P("region", "tp"),
        check_vma=False,
    )
```
